256 devices in a mesh: hb: 4 (over y), row: 16 (over z, x_hi), col: 4 (over x_lo, core).
Axes of the slice: x: 4 (x_hi: 2, x_lo: 2; x = x_hi * 2 + x_lo), y: 4, z: 8, core: 2. Of those that a mesh axis runs over, the one named last changes fastest.
Arguments:
- cell_state: float32 [256, 8, 256, 512], P('hb', None, 'row', 'col'), may hold values from -6 to 6
- normalizer: float32 [256, 8, 256], P('hb', None, 'row'), may hold values from 0.1 to 4
- stabilizer: float32 [256, 8, 16], P('hb', None, 'row'), may hold values from -5 to 120
- queries: float32 [256, 8, 256], P('hb', None, 'row'), may hold values from 0.0125 to 0.1125
- key_vectors: float32 [256, 8, 256], P('hb', None, 'row'), may hold values from -6 to 6
- token_value_vectors: float32 [256, 8, 512], P('hb', None, 'col'), may hold values from -6 to 6
- input_gate: float32 [256, 8], P('hb'), may hold values from -3 to 3
- forget_gate: float32 [256, 8], P('hb'), may hold values from -1 to 5
- output_gate_logits: float32 [256, 8, 512], P('hb', None, 'col'), may hold values from -6 to 6
- norm_gain: float32 [8, 512], P(None, 'col'), may hold values from 0.5 to 1.5
- out_weight: bfloat16 [8, 512, 4096], P('hb', 'col', 'row'), may hold values from -0.09375 to 0.09375
Outputs:
- layer_out: float32 [256, 4096], P('hb', 'row')
- readout: float32 [256, 8, 512], P('hb', None, 'col')
- refreshed_cell: float32 [256, 8, 256, 512], P('hb', None, 'row', 'col')
- new_normal: float32 [256, 8, 256], P('hb', None, 'row')
- new_stab: float32 [256, 8, 16], P('hb', None, 'row')
The draws below stay inside these ranges and needn't reach their ends.
All inputs are finite; a program needn't handle non-finite values.
Results may differ from the reference program's by a relative error of at most 0.0029.
Values may be sent and summed in bfloat16 or wider, within the bound.
No kernel may reach another device: no remote copies, remote signals or barrier semaphores. Data moves between devices by JAX's collectives and lax.ppermute only.
A program may use at most 64 MiB of HBM per device.

```python
import math
import jax
import jax.numpy as jnp
from jax import lax

H = 8
DK = 256
DV = 512
D = 4096
RBLK = 16
NBLK = 16
BATCH = 256


def draw_stabilizer(key, part):
    offset_key, spread_key = jax.random.split(jax.random.fold_in(key, 7))
    offset = jax.random.uniform(offset_key, (BATCH, H, 1), jnp.float32, -1.0, 1.0)
    spread_factor = jax.random.uniform(spread_key, (BATCH, H, NBLK), jnp.float32, -1.5, 1.5)
    return offset + spread_factor


def level_of(rng, extent, shards, least, largest):
    factor_of, own = 1.0, jax.random.fold_in(rng, 6)
    for position, shards_of in shards:
        draws = jnp.exp(jax.random.uniform(jax.random.fold_in(own, position), (shards_of,), jnp.float32, least / len(shards), largest / len(shards)))
        factor_of = factor_of * jnp.repeat(draws, extent[position] // shards_of).reshape([-1 if axis == position else 1 for axis in range(len(extent))])
    return factor_of


def centred(rng, shape, scale, limit, cuts=(), kind=jnp.bfloat16):
    level = level_of(rng, shape, cuts, -0.22, 0.18) if cuts else 1.0
    array = jax.random.normal(rng, shape, jnp.float32) * scale * level
    return jnp.minimum(jnp.maximum(array, -limit), limit).astype(kind)


def setup_inputs(seed: int = 0) -> dict:
    streams_of = jax.random.split(jax.random.key(seed), 12)
    cell_state = centred(streams_of[0], (BATCH, H, DK, DV), 1.0, 6.0, ((0, 4), (2, 16), (3, 4)), jnp.float32)
    normalizer = jnp.clip(jnp.exp(math.log(4.0) - 3.6888794 * jax.random.uniform(streams_of[1], (BATCH, H, DK), jnp.float32) ** level_of(streams_of[1], (BATCH, H, DK), ((0, 4), (2, 16)), -0.2, 0.2)), 0.1, 4.0)
    stabilizer = draw_stabilizer(jax.random.fold_in(streams_of[11], 71), 0)
    queries = jnp.clip(0.0125 + 0.099999997 * jax.random.uniform(streams_of[3], (BATCH, H, DK), jnp.float32) ** level_of(streams_of[3], (BATCH, H, DK), ((0, 4), (2, 16)), -0.2, 0.2), 0.0125, 0.1125)
    key_vectors = centred(streams_of[4], (BATCH, H, DK), 1.0, 6.0, ((0, 4), (2, 16)), jnp.float32)
    token_value_vectors = centred(streams_of[5], (BATCH, H, DV), 1.0, 6.0, ((0, 4), (2, 4)), jnp.float32)
    input_gate = jnp.clip(jax.random.uniform(streams_of[6], (BATCH, H), jnp.float32, -3.0, 3.0) * level_of(streams_of[6], (BATCH, H), ((0, 4),), -0.4, 0.0), -3.0, 3.0)
    forget_gate = jnp.clip(-1.0 + 6.0 * jax.random.uniform(streams_of[7], (BATCH, H), jnp.float32) ** level_of(streams_of[7], (BATCH, H), ((0, 4),), -0.2, 0.2), -1.0, 5.0)
    output_gate_logits = centred(streams_of[8], (BATCH, H, DV), 1.0, 6.0, ((0, 4), (2, 4)), jnp.float32)
    norm_gain = jnp.clip(1.0 + 0.1 * jax.random.normal(streams_of[9], (H, DV), jnp.float32), 0.5, 1.5)
    out_weight = centred(streams_of[10], (H, DV, D), (H * DV) ** -0.5, 0.09375, ((0, 4), (1, 4), (2, 16)))
    return {"cell_state": cell_state, "normalizer": normalizer, "stabilizer": stabilizer, "queries": queries, "key_vectors": key_vectors, "token_value_vectors": token_value_vectors, "input_gate": input_gate, "forget_gate": forget_gate, "output_gate_logits": output_gate_logits, "norm_gain": norm_gain, "out_weight": out_weight}


def advance(cell, normal, stabs, query_row, token_key_row, value_row, in_gate, forget_pre):
    carried = jax.nn.log_sigmoid(forget_pre)[:, None] + stabs
    fresh = jnp.maximum(carried, in_gate[:, None])
    keep = jnp.repeat(jnp.exp(carried - fresh), RBLK, axis=1)
    admit = jnp.repeat(jnp.exp(in_gate[:, None] - fresh), RBLK, axis=1)
    scaled = token_key_row * DK ** (-0.5)
    refreshed_cell = keep[:, :, None] * cell + (admit * scaled)[:, :, None] * value_row[:, None, :]
    new_normal = keep * normal + admit * scaled
    top = lax.optimization_barrier(jnp.max(fresh, axis=1))
    weight_matrix = jnp.repeat(jnp.exp(fresh - top[:, None]), RBLK, axis=1) * query_row
    numerator = jnp.einsum('fdo,fd->fo', refreshed_cell, weight_matrix, precision=lax.Precision.HIGHEST)
    denom = lax.optimization_barrier(jnp.sum(new_normal * weight_matrix, axis=1))
    readout = numerator / jnp.maximum(jnp.abs(denom), jnp.exp(-top))[:, None]
    return (refreshed_cell, new_normal, fresh, readout)

def reference(cell_state, normalizer, stabilizer, queries, key_vectors, token_value_vectors, input_gate, forget_gate, output_gate_logits, norm_gain, out_weight):
    refreshed_cell, new_normal, new_stab, readout = lax.map(lambda packed: advance(*packed), (cell_state, normalizer, stabilizer, queries, key_vectors, token_value_vectors, input_gate, forget_gate))
    mean = lax.optimization_barrier(jnp.sum(readout, axis=2)) / DV
    var = lax.optimization_barrier(jnp.sum(readout * readout, axis=2)) / DV - mean * mean
    normed = (readout - mean[:, :, None]) * lax.rsqrt(var + 1e-06)[:, :, None]
    gated = (normed * norm_gain * jax.nn.sigmoid(output_gate_logits)).astype(jnp.bfloat16)
    layer_out = jnp.dot(gated.reshape(gated.shape[0], H * DV), out_weight.reshape(H * DV, D), preferred_element_type=jnp.float32)
    return (layer_out, readout, refreshed_cell, new_normal, new_stab)
```

```python
import jax
import jax.numpy as jnp
from jax import lax
from jax.experimental import pallas as pl
from jax.experimental.pallas import tpu as pltpu
from jax.sharding import Mesh
from jax.sharding import PartitionSpec as P

H = 8
DK = 256
DV = 512
HB = 4
ROWS = 16
COLS = 4
B = 64
KR = 16
V = 128
OUT = 256
MINE = B // ROWS
NROWS = MINE * H
CHUNK = NROWS + H
NSCALE = 2048.0
DSCALE = 64.0
STEP = 256.0
f32 = jnp.float32
bf16 = jnp.bfloat16
f16 = jnp.float16


def whole(shape):
    return pl.BlockSpec(shape, lambda *_: (0,) * len(shape))


def parts_of(x):
    first = x.astype(bf16).astype(f32)
    rest = (x - first) * STEP
    second = rest.astype(bf16).astype(f32)
    third = (rest - second) * STEP
    return first, second, third


def cell_kernel(
    cell, normal, stab, query, keys, value, in_gate, forget, new_cell, new_normal, new_stab, send,
    keep_s, admit_s, denom_s, numer_s,
):
    h = pl.program_id(0)

    @pl.when(h == 0)
    def _():
        pre = forget[...]
        log_sig = jnp.minimum(pre, 0.0) - jnp.log(1.0 + jnp.exp(-jnp.abs(pre)))
        carried = log_sig + stab[...]
        fresh = jnp.maximum(carried, in_gate[...])
        new_stab[...] = fresh
        keep_s[...] = jnp.exp(carried - fresh)
        admit_s[...] = jnp.exp(in_gate[...] - fresh)

    row = pl.ds(h, 1)
    keep = jnp.broadcast_to(keep_s[row, :], (KR, B))
    add = jnp.broadcast_to(admit_s[row, :], (KR, B)) * (keys[h] * DK**-0.5)
    q = query[h]
    normed = keep * normal[h] + add
    new_normal[h] = normed
    denom_s[row, :] = jnp.sum(q * normed, axis=0, keepdims=True)
    for b in range(B):
        lane = slice(b, b + 1)
        v = jnp.broadcast_to(value[b, row, :], (KR, V))
        fresh_cell = keep[:, lane] * cell[b, 0] + add[:, lane] * v
        new_cell[b, 0] = fresh_cell
        numer_s[b, row, :] = jnp.sum(q[:, lane] * fresh_cell, axis=0, keepdims=True)

    @pl.when(h == H - 1)
    def _():
        fields = parts_of(new_stab[...]) + parts_of(denom_s[...] * DSCALE)
        wide = [jnp.concatenate([x, x], axis=1) for x in fields]
        lanes = lax.broadcasted_iota(jnp.int32, (H, 2 * B), 1)
        for r in range(ROWS):
            tile = jnp.zeros((H, 2 * B), f32)
            for n, x in enumerate(wide):
                shift = (MINE * n - MINE * r) % (2 * B)
                moved = pltpu.roll(x, shift, 1) if shift else x
                inside = (lanes >= MINE * n) & (lanes < MINE * (n + 1))
                tile = jnp.where(inside, moved, tile)
            send[r, NROWS:CHUNK, :] = tile
            for j in range(MINE):
                send[r, H * j : H * (j + 1), :] = numer_s[MINE * r + j] * NSCALE


def combine_kernel(got, out):
    def field(tile, n):
        back = lambda k: pltpu.roll(tile, (-MINE * k) % V, 1) if k else tile
        return back(n) + (back(n + 1) + back(n + 2) * (1.0 / STEP)) * (1.0 / STEP)

    tiles = [got[r, NROWS:CHUNK, :] for r in range(ROWS)]
    stabs = [field(t, 0) for t in tiles]
    top = stabs[0]
    for s in stabs[1:]:
        top = jnp.maximum(top, s)
    scales = [jnp.exp(s - top) for s in stabs]
    denom = scales[0] * field(tiles[0], 3)
    for s, t in zip(scales[1:], tiles[1:]):
        denom = denom + s * field(t, 3)
    base = jnp.maximum(jnp.abs(denom * (1.0 / DSCALE)), jnp.exp(-top)) * NSCALE
    for j in range(MINE):
        lane = slice(j, j + 1)
        rows = slice(H * j, H * (j + 1))
        numer = scales[0][:, lane] * got[0, rows, :]
        for r in range(1, ROWS):
            numer = numer + scales[r][:, lane] * got[r, rows, :]
        readout = (numer / jnp.broadcast_to(base[:, lane], (H, V))).astype(bf16)
        for r in range(ROWS):
            out[r, rows, :] = readout


def stats_kernel(got, readout, stats):
    lanes = lax.broadcasted_iota(jnp.int32, (H, 2 * B), 1)
    tile = jnp.zeros((H, 2 * B), f32)
    for b in range(B):
        x = got[b * H : (b + 1) * H, :].astype(f32)
        readout[b] = x
        total = jnp.sum(x, axis=1, keepdims=True)
        square = jnp.sum(x * x, axis=1, keepdims=True)
        tile = jnp.where(lanes == b, total, tile)
        tile = jnp.where(lanes == B + b, square, tile)
    stats[...] = tile


def project_kernel(me, readout, s0, s1, s2, s3, logits, gain, w0, w1, w2, w3, out, gated):
    total = (s0[...] + s1[...]) + (s2[...] + s3[...])
    mean = total[:, :B] * (1.0 / DV)
    square = total[:, B:] * (1.0 / DV)
    scale = lax.rsqrt(square - mean * mean + 1e-06)
    g = gain[...]
    for b in range(B):
        lane = slice(b, b + 1)
        gate = g / (1.0 + jnp.exp(-logits[b]))
        gated[b * H : (b + 1) * H, :] = (readout[b] - mean[:, lane]) * scale[:, lane] * gate
    acc = jnp.zeros((B, OUT), f32)
    for k, w in enumerate((w0, w1, w2, w3)):
        for j in range(H // HB):
            head = 2 * (me[0] ^ k) + j
            x = gated[pl.ds(head, B, stride=H), :]
            high = x.astype(bf16)
            low = (x - high.astype(f32)).astype(bf16)
            acc = acc + jnp.dot(high, w[j], preferred_element_type=f32)
            acc = acc + jnp.dot(low, w[j], preferred_element_type=f32)
    out[...] = acc


def xor_pairs(n, k):
    return [(i, i ^ k) for i in range(n)]


def local(
    cell_state,
    normalizer,
    stabilizer,
    queries,
    key_vectors,
    token_value_vectors,
    input_gate,
    forget_gate,
    output_gate_logits,
    norm_gain,
    out_weight,
):
    shape = jax.ShapeDtypeStruct
    weights = [out_weight] + [
        lax.ppermute(out_weight, "hb", xor_pairs(HB, k)) for k in range(1, HB)
    ]
    turned = lambda x: jnp.transpose(x, (1, 2, 0))
    cell_block = pl.BlockSpec((B, 1, KR, V), lambda h: (0, h, 0, 0))
    new_cell, new_normal, new_stab, send = pl.pallas_call(
        cell_kernel,
        grid=(H,),
        in_specs=[
            cell_block,
            whole((H, KR, B)),
            whole((H, B)),
            whole((H, KR, B)),
            whole((H, KR, B)),
            whole((B, H, V)),
            whole((H, B)),
            whole((H, B)),
        ],
        out_specs=[cell_block, whole((H, KR, B)), whole((H, B)), whole((ROWS, CHUNK, V))],
        out_shape=[
            shape((B, H, KR, V), f32),
            shape((H, KR, B), f32),
            shape((H, B), f32),
            shape((ROWS, CHUNK, V), f32),
        ],
        scratch_shapes=[
            pltpu.VMEM((H, B), f32),
            pltpu.VMEM((H, B), f32),
            pltpu.VMEM((H, B), f32),
            pltpu.VMEM((B, H, V), f32),
        ],
        name="cell",
    )(
        cell_state,
        turned(normalizer),
        jnp.transpose(stabilizer[:, :, 0]),
        turned(queries),
        turned(key_vectors),
        token_value_vectors,
        jnp.transpose(input_gate),
        jnp.transpose(forget_gate),
    )
    got = lax.all_to_all(send.astype(f16), "row", 0, 0, tiled=True).astype(f32)
    mine = pl.pallas_call(
        combine_kernel, out_shape=shape((ROWS, NROWS, V), bf16), name="combine"
    )(got)
    every = lax.all_to_all(mine, "row", 0, 0, tiled=True)
    readout, stats = pl.pallas_call(
        stats_kernel, out_shape=[shape((B, H, V), f32), shape((H, 2 * B), f32)], name="stats"
    )(every.reshape(B * H, V))
    others = [lax.ppermute(stats, "col", xor_pairs(COLS, k)) for k in range(1, COLS)]
    me = lax.axis_index("hb").astype(jnp.int32).reshape(1)
    vmem = pl.BlockSpec(memory_space=pltpu.VMEM)
    partial_value = pl.pallas_call(
        project_kernel,
        in_specs=[pl.BlockSpec(memory_space=pltpu.SMEM)] + [vmem] * 11,
        out_specs=vmem,
        out_shape=shape((B, OUT), f32),
        scratch_shapes=[pltpu.VMEM((B * H, V), f32)],
        name="project",
    )(me, readout, stats, *others, output_gate_logits, norm_gain, *weights)
    sent = [lax.ppermute(partial_value, "col", xor_pairs(COLS, k)) for k in range(1, COLS)]
    layer_out = (partial_value + sent[0]) + (sent[1] + sent[2])
    return (
        layer_out,
        readout,
        new_cell,
        jnp.transpose(new_normal, (2, 0, 1)),
        jnp.transpose(new_stab)[:, :, None],
    )


def solution(mesh):
    in_specs = (
        P("hb", None, "row", "col"),
        P("hb", None, "row"),
        P("hb", None, "row"),
        P("hb", None, "row"),
        P("hb", None, "row"),
        P("hb", None, "col"),
        P("hb", None),
        P("hb", None),
        P("hb", None, "col"),
        P(None, "col"),
        P("hb", "col", "row"),
    )
    out_specs = (
        P("hb", "row"),
        P("hb", None, "col"),
        P("hb", None, "row", "col"),
        P("hb", None, "row"),
        P("hb", None, "row"),
    )
    return jax.shard_map(local, mesh=mesh, in_specs=in_specs, out_specs=out_specs, check_vma=False)
```

```python
import functools

import jax
import jax.numpy as jnp
from jax import lax
from jax.experimental import pallas as pl
from jax.experimental.pallas import tpu as pltpu
from jax.sharding import PartitionSpec as P

H = 8
DK = 256
DV = 512
HB = 4
ROWS = 16
COLS = 4
B = 64
KR = 16
V = 128
OUT = 256
MINE = B // ROWS
BLOCK = 8
NROWS = MINE * H
CHUNK = NROWS + H
NSCALE = 2048.0
DSCALE = 64.0
OSCALE = 64.0
STEP = 256.0
READ_KIB = 65152
WRITE_KIB = 60 * 1024
f32 = jnp.float32
bf16 = jnp.bfloat16
f16 = jnp.float16


def parts_of(x):
    first = x.astype(bf16).astype(f32)
    rest = (x - first) * STEP
    second = rest.astype(bf16).astype(f32)
    third = (rest - second) * STEP
    return first, second, third


def gates(stab, in_gate, forget):
    pre = forget[...]
    log_sig = jnp.minimum(pre, 0.0) - jnp.log(1.0 + jnp.exp(-jnp.abs(pre)))
    carried = log_sig + stab[...]
    fresh = jnp.maximum(carried, in_gate[...])
    return fresh, jnp.exp(carried - fresh), jnp.exp(in_gate[...] - fresh) * DK**-0.5


def over_rows(x, h):
    return jnp.broadcast_to(x[h : h + 1, :], (KR, B))


def fetches(sems, *pairs):
    return [pltpu.make_async_copy(a, b, sems.at[n]) for n, (a, b) in enumerate(pairs)]


def cell_rows(step, count=1):
    return pl.ds(pl.multiple_of(BLOCK * H * KR * step, BLOCK * H * KR), BLOCK * H * KR * count)


def read_kernel(
    cell_h, normal_h, stab_h, query_h, keys_h, value_h, in_gate_h, forget_h,
    new_normal, new_stab, send,
    cell, normal, stab, query, keys, value, in_gate, forget,
    keep_s, mixed_s, high_s, low_s, field_s, sems, cell_sems,
):
    small = fetches(
        sems, (stab_h, stab), (in_gate_h, in_gate), (forget_h, forget), (keys_h, keys),
        (query_h, query), (normal_h, normal), (value_h, value),
    )
    large = [
        pltpu.make_async_copy(cell_h.at[cell_rows(n)], cell.at[cell_rows(n)], cell_sems.at[n])
        for n in range(B // BLOCK)
    ]
    for c in small + large:
        c.start()
    for c in small:
        c.wait()
    read_start(
        normal, stab, query, keys, in_gate, forget, new_normal, new_stab,
        keep_s, mixed_s, high_s, low_s, field_s,
    )

    def body(step, carry):
        pltpu.make_async_copy(
            cell_h.at[cell_rows(step)], cell.at[cell_rows(step)], cell_sems.at[step]
        ).wait()
        read_step(step, cell, value, send, keep_s, mixed_s, high_s, low_s, field_s)
        return carry

    lax.fori_loop(0, B // BLOCK, body, 0)


def read_start(
    normal, stab, query, keys, in_gate, forget, new_normal, new_stab,
    keep_s, mixed_s, high_s, low_s, field_s,
):
    fresh, keep, admit = gates(stab, in_gate, forget)
    new_stab[...] = fresh
    keep_s[:, :B] = keep
    heads = lax.broadcasted_iota(jnp.int32, (H, B), 0)
    denom = jnp.zeros((H, B), f32)
    mixed = jnp.zeros((H, B), f32)
    for h in range(H):
        rows = slice(KR * h, KR * (h + 1))
        add = over_rows(admit, h) * keys[rows, :]
        q = query[rows, :]
        normed = over_rows(keep, h) * normal[rows, :] + add
        new_normal[rows, :] = normed
        denom = jnp.where(heads == h, jnp.sum(q * normed, axis=0, keepdims=True), denom)
        mixed = jnp.where(heads == h, jnp.sum(q * add, axis=0, keepdims=True), mixed)
    mixed_s[:, :B] = mixed
    for n, x in enumerate(parts_of(fresh) + parts_of(denom * DSCALE)):
        field_s[n, :, :B] = x
    q = jnp.transpose(jnp.concatenate([query[...], query[...]], axis=1))[:B, :]
    high = q.astype(bf16).astype(f32)
    high_s[...] = high
    low_s[...] = q - high


def read_step(step, cell, value, send, keep_s, mixed_s, high_s, low_s, field_s):
    back = lax.rem(2 * B - BLOCK * step, 2 * B)
    keep = pltpu.roll(keep_s[...], back, 1)
    mixed = pltpu.roll(mixed_s[...], back, 1)
    heads = lax.broadcasted_iota(jnp.int32, (H, V), 0)
    own = lax.broadcasted_iota(jnp.int32, (H, V), 1) // KR == heads
    for b in range(BLOCK):
        lane = slice(b, b + 1)
        row = pl.ds(BLOCK * step + b, 1)
        high = jnp.where(own, jnp.broadcast_to(high_s[row, :], (H, V)), 0.0)
        low = jnp.where(own, jnp.broadcast_to(low_s[row, :], (H, V)), 0.0)
        q = jnp.concatenate([high, low], axis=0).astype(bf16)
        start = pl.multiple_of((BLOCK * step + b) * H * KR, H * KR)
        held = cell[pl.ds(start, H * KR), :]
        first = held.astype(bf16)
        second = (held - first.astype(f32)).astype(bf16)
        total = jnp.dot(q, first, preferred_element_type=f32)
        total = total + jnp.dot(q, second, preferred_element_type=f32)
        numer = keep[:, lane] * (total[:H] + total[H:]) + mixed[:, lane] * value[BLOCK * step + b]
        at = (BLOCK // MINE) * step + b // MINE
        j = b % MINE
        send[at, H * j : H * (j + 1), :] = numer * NSCALE

    lanes = lax.broadcasted_iota(jnp.int32, (H, 2 * B), 1)
    for c in range(BLOCK // MINE):
        tile = jnp.zeros((H, 2 * B), f32)
        for n in range(6):
            shift = lax.rem(back + (MINE * (n - c)) % (2 * B), 2 * B)
            inside = (lanes >= MINE * n) & (lanes < MINE * (n + 1))
            tile = jnp.where(inside, pltpu.roll(field_s[n], shift, 1), tile)
        send[(BLOCK // MINE) * step + c, NROWS:CHUNK, :] = tile


def halves(x):
    high = x.astype(bf16).astype(f32)
    return jnp.concatenate([high, x - high], axis=1)


def write_kernel(first, steps, cell_h, stab_h, keys_h, value_h, in_gate_h, forget_h, *rest):
    (new_cell_h, cell, new_cell, stab, keys, value, in_gate, forget, factors_s,
     sems, in_sems, out_sems) = rest[-12:]
    seqs = pl.ds(BLOCK * first, BLOCK * steps)
    small = fetches(
        sems, (stab_h, stab), (in_gate_h, in_gate), (forget_h, forget), (keys_h, keys),
        (value_h.at[seqs], value),
    )
    large = [
        pltpu.make_async_copy(cell_h.at[cell_rows(first + n)], cell.at[cell_rows(n)], in_sems.at[n])
        for n in range(steps)
    ]
    for c in small + large:
        c.start()
    for c in small:
        c.wait()
    _, held, admit = gates(stab, in_gate, forget)
    for h in range(H):
        factors_s[KR * h : KR * (h + 1), :] = halves(over_rows(admit, h) * keys[KR * h : KR * (h + 1), :])
        keep = jnp.broadcast_to(held[h : h + 1, :], (8, B))
        factors_s[H * KR + 8 * h : H * KR + 8 * (h + 1), :] = halves(keep)
    factors = factors_s[...].astype(bf16)
    places = lax.rem(lax.broadcasted_iota(jnp.int32, (2 * B, V), 0), B)

    def body(n, carry):
        pltpu.make_async_copy(
            cell_h.at[cell_rows(first + n)], cell.at[cell_rows(n)], in_sems.at[n]
        ).wait()
        for b in range(BLOCK):
            seq = BLOCK * n + b
            pick = jnp.where(places == BLOCK * first + seq, 1.0, 0.0).astype(bf16)
            spread = jnp.dot(factors, pick, preferred_element_type=f32)
            for h in range(H):
                keep = spread[H * KR + 8 * h : H * KR + 8 * (h + 1), :]
                v = value[seq, h : h + 1, :]
                for t in range(KR * h, KR * (h + 1), 8):
                    rows = pl.ds(pl.multiple_of(seq * H * KR + t, 8), 8)
                    new_cell[rows, :] = keep * cell[rows, :] + spread[t : t + 8, :] * v
        pltpu.make_async_copy(
            new_cell.at[cell_rows(n)], new_cell_h.at[cell_rows(first + n)], out_sems.at[n]
        ).start()
        return carry

    lax.fori_loop(0, steps, body, 0)
    for n in range(steps):
        pltpu.make_async_copy(
            new_cell.at[cell_rows(n)], new_cell_h.at[cell_rows(first + n)], out_sems.at[n]
        ).wait()


def combine_kernel(got, out):
    def field(tile, n):
        back = lambda k: pltpu.roll(tile, (-MINE * k) % V, 1) if k else tile
        return back(n) + (back(n + 1) + back(n + 2) * (1.0 / STEP)) * (1.0 / STEP)

    tiles = [got[r, NROWS:CHUNK, :] for r in range(ROWS)]
    stabs = [field(t, 0) for t in tiles]
    top = stabs[0]
    for s in stabs[1:]:
        top = jnp.maximum(top, s)
    scales = [jnp.exp(s - top) for s in stabs]
    denom = scales[0] * field(tiles[0], 3)
    for s, t in zip(scales[1:], tiles[1:]):
        denom = denom + s * field(t, 3)
    base = jnp.maximum(jnp.abs(denom * (1.0 / DSCALE)), jnp.exp(-top)) * NSCALE
    for j in range(MINE):
        lane = slice(j, j + 1)
        rows = slice(H * j, H * (j + 1))
        numer = scales[0][:, lane] * got[0, rows, :]
        for r in range(1, ROWS):
            numer = numer + scales[r][:, lane] * got[r, rows, :]
        readout = (numer / jnp.broadcast_to(base[:, lane], (H, V))).astype(bf16)
        for r in range(ROWS):
            out[r, rows, :] = readout


def stats_kernel(got, readout, stats):
    lanes = lax.broadcasted_iota(jnp.int32, (H, 2 * B), 1)
    tile = jnp.zeros((H, 2 * B), f32)
    for b in range(B):
        x = got[b * H : (b + 1) * H, :].astype(f32)
        readout[b] = x
        total = jnp.sum(x, axis=1, keepdims=True)
        square = jnp.sum(x * x, axis=1, keepdims=True)
        tile = jnp.where(lanes == b, total, tile)
        tile = jnp.where(lanes == B + b, square, tile)
    stats[...] = tile


def gate_kernel(logits, gain, weight, out, weight_out):
    g = gain[...]
    for b in range(B):
        out[b] = g / (1.0 + jnp.exp(-logits[b]))
    weight_out[...] = weight[...]


def project_kernel(me, got, stats, gate, w0, w1, w2, w3, out, gated):
    total = ((stats[0] + stats[1]) + (stats[2] + stats[3])) * (1.0 / DV)
    square = pltpu.roll(total, B, 1)
    scale = lax.rsqrt(square - total * total + 1e-06)
    for b in range(B):
        lane = slice(b, b + 1)
        rows = slice(b * H, (b + 1) * H)
        gated[rows, :] = (got[rows, :].astype(f32) - total[:, lane]) * (scale[:, lane] * gate[b])
    acc = jnp.zeros((B, OUT), f32)
    for k, w in enumerate((w0, w1, w2, w3)):
        for j in range(H // HB):
            head = 2 * (me[0] ^ k) + j
            x = gated[pl.ds(head, B, stride=H), :]
            high = x.astype(bf16)
            low = (x - high.astype(f32)).astype(bf16)
            acc = acc + jnp.dot(high, w[j], preferred_element_type=f32)
            acc = acc + jnp.dot(low, w[j], preferred_element_type=f32)
    out[...] = acc * OSCALE


def xor_pairs(n, k):
    return [(i, i ^ k) for i in range(n)]


def local(
    cell_state,
    normalizer,
    stabilizer,
    queries,
    key_vectors,
    token_value_vectors,
    input_gate,
    forget_gate,
    output_gate_logits,
    norm_gain,
    out_weight,
):
    shape = jax.ShapeDtypeStruct
    vmem = pl.BlockSpec(memory_space=pltpu.VMEM)
    weights = [out_weight]
    for k in (1, 2, 3):
        weights.append(lax.ppermute(out_weight, "hb", xor_pairs(HB, k)))
    turned = lambda x: jnp.transpose(x, (1, 2, 0)).reshape(H * KR, B)
    cells = cell_state.reshape(B * H * KR, V)
    stab = jnp.transpose(stabilizer[:, :, 0])
    keys = turned(key_vectors)
    in_gate = jnp.transpose(input_gate)
    forget = jnp.transpose(forget_gate)
    anywhere = pl.BlockSpec(memory_space=pl.ANY)
    rows_s = pltpu.VMEM((H * KR, B), f32)
    gate_s = pltpu.VMEM((H, B), f32)
    new_normal, new_stab, send = pl.pallas_call(
        read_kernel,
        in_specs=[anywhere] * 8,
        out_specs=[vmem] * 3,
        out_shape=[
            shape((H * KR, B), f32),
            shape((H, B), f32),
            shape((ROWS, CHUNK, V), f32),
        ],
        scratch_shapes=[
            pltpu.VMEM((B * H * KR, V), f32),
            rows_s,
            gate_s,
            rows_s,
            rows_s,
            pltpu.VMEM((B, H, V), f32),
            gate_s,
            gate_s,
            pltpu.VMEM((H, 2 * B), f32),
            pltpu.VMEM((H, 2 * B), f32),
            pltpu.VMEM((B, V), f32),
            pltpu.VMEM((B, V), f32),
            pltpu.VMEM((6, H, 2 * B), f32),
            pltpu.SemaphoreType.DMA((7,)),
            pltpu.SemaphoreType.DMA((B // BLOCK,)),
        ],
        name="read",
        compiler_params=pltpu.CompilerParams(vmem_limit_bytes=READ_KIB << 10),
    )(cells, turned(normalizer), stab, turned(queries), keys, token_value_vectors, in_gate, forget)

    def written(first, steps, *before):
        size = BLOCK * steps
        return pl.pallas_call(
            functools.partial(write_kernel, first, steps),
            in_specs=[anywhere] * (6 + len(before)),
            out_specs=anywhere,
            out_shape=shape((B * H * KR, V), f32),
            scratch_shapes=[
                pltpu.VMEM((size * H * KR, V), f32),
                pltpu.VMEM((size * H * KR, V), f32),
                gate_s,
                rows_s,
                pltpu.VMEM((size, H, V), f32),
                gate_s,
                gate_s,
                pltpu.VMEM((H * KR + 8 * H, 2 * B), f32),
                pltpu.SemaphoreType.DMA((5,)),
                pltpu.SemaphoreType.DMA((steps,)),
                pltpu.SemaphoreType.DMA((steps,)),
            ],
            input_output_aliases={6: 0} if before else {},
            compiler_params=pltpu.CompilerParams(vmem_limit_bytes=WRITE_KIB << 10),
            cost_estimate=pl.CostEstimate(flops=0, bytes_accessed=steps << 20, transcendentals=0),
        )(cells, stab, keys, token_value_vectors, in_gate, forget, *before)

    half = B // BLOCK // 2
    new_cell = written(0, half)
    new_cell = written(half, half, new_cell)
    send = send.astype(f16)
    got = lax.all_to_all(send, "row", 0, 0, tiled=True)
    got = got.astype(f32)
    mine = pl.pallas_call(
        combine_kernel,
        in_specs=[vmem],
        out_specs=vmem,
        out_shape=shape((ROWS, NROWS, V), bf16),
        name="combine",
        compiler_params=pltpu.CompilerParams(vmem_limit_bytes=4 << 20),
    )(got)
    every = lax.all_to_all(mine, "row", 0, 0, tiled=True)
    every = every.reshape(B * H, V)
    gate, weights[0] = pl.pallas_call(
        gate_kernel,
        in_specs=[vmem] * 3,
        out_specs=[vmem] * 2,
        out_shape=[shape((B, H, V), f32), shape(out_weight.shape, bf16)],
        name="gate",
        compiler_params=pltpu.CompilerParams(vmem_limit_bytes=4 << 20),
    )(output_gate_logits, norm_gain, out_weight)
    readout, stats = pl.pallas_call(
        stats_kernel,
        in_specs=[vmem],
        out_specs=[vmem] * 2,
        out_shape=[shape((B, H, V), f32), shape((H, 2 * B), f32)],
        name="stats",
        compiler_params=pltpu.CompilerParams(vmem_limit_bytes=4 << 20),
    )(every)
    stats = lax.all_gather(stats, "col")
    me = lax.axis_index("hb").astype(jnp.int32).reshape(1)
    partial_value = pl.pallas_call(
        project_kernel,
        in_specs=[pl.BlockSpec(memory_space=pltpu.SMEM)] + [vmem] * 7,
        out_specs=vmem,
        out_shape=shape((B, OUT), f32),
        scratch_shapes=[pltpu.VMEM((B * H, V), f32)],
        name="project",
        compiler_params=pltpu.CompilerParams(vmem_limit_bytes=6 << 20),
    )(me, every, stats, gate, *weights)
    sent = [lax.optimization_barrier(partial_value.astype(f16))]
    for k in range(1, COLS):
        sent.append(lax.ppermute(sent[0], "col", xor_pairs(COLS, k)))
    sent = [x.astype(f32) for x in sent]
    layer_out = ((sent[0] + sent[1]) + (sent[2] + sent[3])) * (1.0 / OSCALE)
    return (
        layer_out,
        readout,
        new_cell.reshape(B, H, KR, V),
        jnp.transpose(new_normal.reshape(H, KR, B), (2, 0, 1)),
        jnp.transpose(new_stab)[:, :, None],
    )


def solution(mesh):
    in_specs = (
        P("hb", None, "row", "col"),
        P("hb", None, "row"),
        P("hb", None, "row"),
        P("hb", None, "row"),
        P("hb", None, "row"),
        P("hb", None, "col"),
        P("hb", None),
        P("hb", None),
        P("hb", None, "col"),
        P(None, "col"),
        P("hb", "col", "row"),
    )
    out_specs = (
        P("hb", "row"),
        P("hb", None, "col"),
        P("hb", None, "row", "col"),
        P("hb", None, "row"),
        P("hb", None, "row"),
    )
    return jax.shard_map(local, mesh=mesh, in_specs=in_specs, out_specs=out_specs, check_vma=False)
```

```python
import functools

import jax
import jax.numpy as jnp
from jax import lax
from jax.experimental import pallas as pl
from jax.experimental.pallas import tpu as pltpu
from jax.sharding import PartitionSpec as P

H = 8
DK = 256
DV = 512
HB = 4
ROWS = 16
COLS = 4
B = 64
KR = 16
V = 128
OUT = 256
MINE = B // ROWS
BLOCK = 8
NROWS = MINE * H
CHUNK = NROWS + H
NSCALE = 2048.0
DSCALE = 64.0
OSCALE = 64.0
STEP = 256.0
READ_KIB = 65152
WRITE_KIB = 60 * 1024
f32 = jnp.float32
bf16 = jnp.bfloat16
f16 = jnp.float16


def parts_of(x):
    first = x.astype(bf16).astype(f32)
    rest = (x - first) * STEP
    second = rest.astype(bf16).astype(f32)
    third = (rest - second) * STEP
    return first, second, third


def gates(stab, in_gate, forget):
    pre = forget[...]
    log_sig = jnp.minimum(pre, 0.0) - jnp.log(1.0 + jnp.exp(-jnp.abs(pre)))
    carried = log_sig + stab[...]
    fresh = jnp.maximum(carried, in_gate[...])
    return fresh, jnp.exp(carried - fresh), jnp.exp(in_gate[...] - fresh) * DK**-0.5


def over_rows(x, h):
    return jnp.broadcast_to(x[h : h + 1, :], (KR, B))


def fetches(sems, *pairs):
    return [pltpu.make_async_copy(a, b, sems.at[n]) for n, (a, b) in enumerate(pairs)]


def cell_rows(step, count=1):
    return pl.ds(pl.multiple_of(BLOCK * H * KR * step, BLOCK * H * KR), BLOCK * H * KR * count)


def read_kernel(
    cell_h, normal_h, stab_h, query_h, keys_h, value_h, in_gate_h, forget_h,
    new_normal, new_stab, send,
    cell, normal, stab, query, keys, value, in_gate, forget,
    keep_s, mixed_s, high_s, low_s, sems, cell_sems,
):
    small = fetches(
        sems, (stab_h, stab), (in_gate_h, in_gate), (forget_h, forget), (keys_h, keys),
        (query_h, query), (normal_h, normal), (value_h, value),
    )
    large = [
        pltpu.make_async_copy(cell_h.at[cell_rows(n)], cell.at[cell_rows(n)], cell_sems.at[n])
        for n in range(B // BLOCK)
    ]
    for c in small + large:
        c.start()
    for c in small:
        c.wait()
    read_start(
        normal, stab, query, keys, in_gate, forget, new_normal, new_stab, send,
        keep_s, mixed_s, high_s, low_s,
    )

    def body(step, carry):
        pltpu.make_async_copy(
            cell_h.at[cell_rows(step)], cell.at[cell_rows(step)], cell_sems.at[step]
        ).wait()
        read_step(step, cell, value, send, keep_s, mixed_s, high_s, low_s)
        return carry

    lax.fori_loop(0, B // BLOCK, body, 0)


def read_start(
    normal, stab, query, keys, in_gate, forget, new_normal, new_stab, send,
    keep_s, mixed_s, high_s, low_s,
):
    fresh, keep, admit = gates(stab, in_gate, forget)
    new_stab[...] = fresh
    keep_s[:, :B] = keep
    heads = lax.broadcasted_iota(jnp.int32, (H, B), 0)
    denom = jnp.zeros((H, B), f32)
    mixed = jnp.zeros((H, B), f32)
    for h in range(H):
        rows = slice(KR * h, KR * (h + 1))
        add = over_rows(admit, h) * keys[rows, :]
        q = query[rows, :]
        normed = over_rows(keep, h) * normal[rows, :] + add
        new_normal[rows, :] = normed
        denom = jnp.where(heads == h, jnp.sum(q * normed, axis=0, keepdims=True), denom)
        mixed = jnp.where(heads == h, jnp.sum(q * add, axis=0, keepdims=True), mixed)
    mixed_s[:, :B] = mixed
    fields = parts_of(fresh) + parts_of(denom * DSCALE)
    count = len(fields)
    groups = lax.broadcasted_iota(jnp.int32, (H, 2 * B), 1) // MINE
    wide = [jnp.concatenate([x, jnp.zeros_like(x)], axis=1) for x in fields]
    wide = [pltpu.roll(x, MINE * n, 1) if n else x for n, x in enumerate(wide)]
    for first in range(count):
        packed = wide[0]
        for n in range(1, count):
            packed = jnp.where(lax.rem(groups + (count - first), count) == n, wide[n], packed)
        for r in range(first, ROWS, count):
            tile = pltpu.roll(packed, 2 * B - MINE * r, 1) if r else packed
            send[r, NROWS:CHUNK, :] = tile
    q = jnp.transpose(jnp.concatenate([query[...], query[...]], axis=1))[:B, :]
    high = q.astype(bf16).astype(f32)
    high_s[...] = high
    low_s[...] = q - high


def read_step(step, cell, value, send, keep_s, mixed_s, high_s, low_s):
    back = lax.rem(2 * B - BLOCK * step, 2 * B)
    keep = pltpu.roll(keep_s[...], back, 1)
    mixed = pltpu.roll(mixed_s[...], back, 1)
    heads = lax.broadcasted_iota(jnp.int32, (H, V), 0)
    own = lax.broadcasted_iota(jnp.int32, (H, V), 1) // KR == heads
    for b in range(BLOCK):
        lane = slice(b, b + 1)
        row = pl.ds(BLOCK * step + b, 1)
        high = jnp.where(own, jnp.broadcast_to(high_s[row, :], (H, V)), 0.0)
        low = jnp.where(own, jnp.broadcast_to(low_s[row, :], (H, V)), 0.0)
        q = jnp.concatenate([high, low], axis=0).astype(bf16)
        start = pl.multiple_of((BLOCK * step + b) * H * KR, H * KR)
        held = cell[pl.ds(start, H * KR), :]
        first = held.astype(bf16)
        second = (held - first.astype(f32)).astype(bf16)
        total = jnp.dot(q, first, preferred_element_type=f32)
        total = total + jnp.dot(q, second, preferred_element_type=f32)
        numer = keep[:, lane] * (total[:H] + total[H:]) + mixed[:, lane] * value[BLOCK * step + b]
        at = (BLOCK // MINE) * step + b // MINE
        j = b % MINE
        send[at, H * j : H * (j + 1), :] = numer * NSCALE


def halves(x):
    high = x.astype(bf16).astype(f32)
    return jnp.concatenate([high, x - high], axis=1)


def write_kernel(first, steps, cell_h, stab_h, keys_h, value_h, in_gate_h, forget_h, *rest):
    (new_cell_h, cell, new_cell, stab, keys, value, in_gate, forget, factors_s,
     sems, in_sems, out_sems) = rest[-12:]
    seqs = pl.ds(BLOCK * first, BLOCK * steps)
    small = fetches(
        sems, (stab_h, stab), (in_gate_h, in_gate), (forget_h, forget), (keys_h, keys),
        (value_h.at[seqs], value),
    )
    large = [
        pltpu.make_async_copy(cell_h.at[cell_rows(first + n)], cell.at[cell_rows(n)], in_sems.at[n])
        for n in range(steps)
    ]
    for c in small + large:
        c.start()
    for c in small:
        c.wait()
    _, held, admit = gates(stab, in_gate, forget)
    for h in range(H):
        factors_s[KR * h : KR * (h + 1), :] = halves(over_rows(admit, h) * keys[KR * h : KR * (h + 1), :])
        keep = jnp.broadcast_to(held[h : h + 1, :], (8, B))
        factors_s[H * KR + 8 * h : H * KR + 8 * (h + 1), :] = halves(keep)
    factors = factors_s[...].astype(bf16)
    places = lax.rem(lax.broadcasted_iota(jnp.int32, (2 * B, V), 0), B)

    def body(n, carry):
        pltpu.make_async_copy(
            cell_h.at[cell_rows(first + n)], cell.at[cell_rows(n)], in_sems.at[n]
        ).wait()
        for b in range(BLOCK):
            seq = BLOCK * n + b
            pick = jnp.where(places == BLOCK * first + seq, 1.0, 0.0).astype(bf16)
            spread = jnp.dot(factors, pick, preferred_element_type=f32)
            for h in range(H):
                keep = spread[H * KR + 8 * h : H * KR + 8 * (h + 1), :]
                v = value[seq, h : h + 1, :]
                for t in range(KR * h, KR * (h + 1), 8):
                    rows = pl.ds(pl.multiple_of(seq * H * KR + t, 8), 8)
                    new_cell[rows, :] = keep * cell[rows, :] + spread[t : t + 8, :] * v
        pltpu.make_async_copy(
            new_cell.at[cell_rows(n)], new_cell_h.at[cell_rows(first + n)], out_sems.at[n]
        ).start()
        return carry

    lax.fori_loop(0, steps, body, 0)
    for n in range(steps):
        pltpu.make_async_copy(
            new_cell.at[cell_rows(n)], new_cell_h.at[cell_rows(first + n)], out_sems.at[n]
        ).wait()


def combine_kernel(got, out):
    def field(tile, n):
        back = lambda k: pltpu.roll(tile, (-MINE * k) % V, 1) if k else tile
        return back(n) + (back(n + 1) + back(n + 2) * (1.0 / STEP)) * (1.0 / STEP)

    tiles = [got[r, NROWS:CHUNK, :] for r in range(ROWS)]
    stabs = [field(t, 0) for t in tiles]
    top = stabs[0]
    for s in stabs[1:]:
        top = jnp.maximum(top, s)
    scales = [jnp.exp(s - top) for s in stabs]
    denom = scales[0] * field(tiles[0], 3)
    for s, t in zip(scales[1:], tiles[1:]):
        denom = denom + s * field(t, 3)
    base = jnp.maximum(jnp.abs(denom * (1.0 / DSCALE)), jnp.exp(-top)) * NSCALE
    for j in range(MINE):
        lane = slice(j, j + 1)
        rows = slice(H * j, H * (j + 1))
        numer = scales[0][:, lane] * got[0, rows, :]
        for r in range(1, ROWS):
            numer = numer + scales[r][:, lane] * got[r, rows, :]
        readout = (numer / jnp.broadcast_to(base[:, lane], (H, V))).astype(bf16)
        for r in range(ROWS):
            out[r, rows, :] = readout


def stats_kernel(got, readout, stats):
    lanes = lax.broadcasted_iota(jnp.int32, (H, 2 * B), 1)
    tile = jnp.zeros((H, 2 * B), f32)
    for b in range(B):
        x = got[b * H : (b + 1) * H, :].astype(f32)
        readout[b] = x
        total = jnp.sum(x, axis=1, keepdims=True)
        square = jnp.sum(x * x, axis=1, keepdims=True)
        tile = jnp.where(lanes == b, total, tile)
        tile = jnp.where(lanes == B + b, square, tile)
    stats[...] = tile


def gate_kernel(logits, gain, weight, out, weight_out):
    g = gain[...]
    for b in range(B):
        out[b] = g / (1.0 + jnp.exp(-logits[b]))
    weight_out[...] = weight[...]


def project_kernel(me, got, s0, s1, s2, s3, gate, w0, w1, w2, w3, out, gated):
    total = ((s0[...] + s1[...]) + (s2[...] + s3[...])) * (1.0 / DV)
    square = pltpu.roll(total, B, 1)
    scale = lax.rsqrt(square - total * total + 1e-06)
    for b in range(B):
        lane = slice(b, b + 1)
        rows = slice(b * H, (b + 1) * H)
        gated[rows, :] = (got[rows, :].astype(f32) - total[:, lane]) * (scale[:, lane] * gate[b])
    acc = jnp.zeros((B, OUT), f32)
    for k, w in enumerate((w0, w1, w2, w3)):
        for j in range(H // HB):
            head = 2 * (me[0] ^ k) + j
            x = gated[pl.ds(head, B, stride=H), :]
            high = x.astype(bf16)
            low = (x - high.astype(f32)).astype(bf16)
            acc = acc + jnp.dot(high, w[j], preferred_element_type=f32)
            acc = acc + jnp.dot(low, w[j], preferred_element_type=f32)
    out[...] = acc * OSCALE


def xor_pairs(n, k):
    return [(i, i ^ k) for i in range(n)]


def local(
    cell_state,
    normalizer,
    stabilizer,
    queries,
    key_vectors,
    token_value_vectors,
    input_gate,
    forget_gate,
    output_gate_logits,
    norm_gain,
    out_weight,
):
    shape = jax.ShapeDtypeStruct
    vmem = pl.BlockSpec(memory_space=pltpu.VMEM)
    weights = [out_weight]
    for k in (1, 2, 3):
        weights.append(lax.ppermute(out_weight, "hb", xor_pairs(HB, k)))
    turned = lambda x: jnp.transpose(x, (1, 2, 0)).reshape(H * KR, B)
    cells = cell_state.reshape(B * H * KR, V)
    stab = jnp.transpose(stabilizer[:, :, 0])
    keys = turned(key_vectors)
    in_gate = jnp.transpose(input_gate)
    forget = jnp.transpose(forget_gate)
    anywhere = pl.BlockSpec(memory_space=pl.ANY)
    rows_s = pltpu.VMEM((H * KR, B), f32)
    gate_s = pltpu.VMEM((H, B), f32)
    new_normal, new_stab, send = pl.pallas_call(
        read_kernel,
        in_specs=[anywhere] * 8,
        out_specs=[vmem] * 3,
        out_shape=[
            shape((H * KR, B), f32),
            shape((H, B), f32),
            shape((ROWS, CHUNK, V), f32),
        ],
        scratch_shapes=[
            pltpu.VMEM((B * H * KR, V), f32),
            rows_s,
            gate_s,
            rows_s,
            rows_s,
            pltpu.VMEM((B, H, V), f32),
            gate_s,
            gate_s,
            pltpu.VMEM((H, 2 * B), f32),
            pltpu.VMEM((H, 2 * B), f32),
            pltpu.VMEM((B, V), f32),
            pltpu.VMEM((B, V), f32),
            pltpu.SemaphoreType.DMA((7,)),
            pltpu.SemaphoreType.DMA((B // BLOCK,)),
        ],
        name="read",
        compiler_params=pltpu.CompilerParams(vmem_limit_bytes=READ_KIB << 10),
    )(cells, turned(normalizer), stab, turned(queries), keys, token_value_vectors, in_gate, forget)

    def written(first, steps, *before):
        size = BLOCK * steps
        return pl.pallas_call(
            functools.partial(write_kernel, first, steps),
            in_specs=[anywhere] * (6 + len(before)),
            out_specs=anywhere,
            out_shape=shape((B * H * KR, V), f32),
            scratch_shapes=[
                pltpu.VMEM((size * H * KR, V), f32),
                pltpu.VMEM((size * H * KR, V), f32),
                gate_s,
                rows_s,
                pltpu.VMEM((size, H, V), f32),
                gate_s,
                gate_s,
                pltpu.VMEM((H * KR + 8 * H, 2 * B), f32),
                pltpu.SemaphoreType.DMA((5,)),
                pltpu.SemaphoreType.DMA((steps,)),
                pltpu.SemaphoreType.DMA((steps,)),
            ],
            input_output_aliases={6: 0} if before else {},
            compiler_params=pltpu.CompilerParams(vmem_limit_bytes=WRITE_KIB << 10),
            cost_estimate=pl.CostEstimate(flops=0, bytes_accessed=steps << 20, transcendentals=0),
        )(cells, stab, keys, token_value_vectors, in_gate, forget, *before)

    half = B // BLOCK // 2
    new_cell = written(0, half + half // 2)
    new_cell = written(half + half // 2, half // 2, new_cell)
    send = send.astype(f16)
    got = lax.all_to_all(send, "row", 0, 0, tiled=True)
    got = got.astype(f32)
    mine = pl.pallas_call(
        combine_kernel,
        in_specs=[vmem],
        out_specs=vmem,
        out_shape=shape((ROWS, NROWS, V), bf16),
        name="combine",
        compiler_params=pltpu.CompilerParams(vmem_limit_bytes=4 << 20),
    )(got)
    every = lax.all_to_all(mine, "row", 0, 0, tiled=True)
    every = every.reshape(B * H, V)
    gate, weights[0] = pl.pallas_call(
        gate_kernel,
        in_specs=[vmem] * 3,
        out_specs=[vmem] * 2,
        out_shape=[shape((B, H, V), f32), shape(out_weight.shape, bf16)],
        name="gate",
        compiler_params=pltpu.CompilerParams(vmem_limit_bytes=4 << 20),
    )(output_gate_logits, norm_gain, out_weight)
    readout, stats = pl.pallas_call(
        stats_kernel,
        in_specs=[vmem],
        out_specs=[vmem] * 2,
        out_shape=[shape((B, H, V), f32), shape((H, 2 * B), f32)],
        name="stats",
        compiler_params=pltpu.CompilerParams(vmem_limit_bytes=4 << 20),
    )(every)
    stats = [stats]
    for k in range(1, COLS):
        stats.append(lax.ppermute(stats[0], "col", xor_pairs(COLS, k)))
    me = lax.axis_index("hb").astype(jnp.int32).reshape(1)
    partial_value = pl.pallas_call(
        project_kernel,
        in_specs=[pl.BlockSpec(memory_space=pltpu.SMEM)] + [vmem] * 10,
        out_specs=vmem,
        out_shape=shape((B, OUT), f32),
        scratch_shapes=[pltpu.VMEM((B * H, V), f32)],
        name="project",
        compiler_params=pltpu.CompilerParams(vmem_limit_bytes=6 << 20),
    )(me, every, *stats, gate, *weights)
    sent = [lax.optimization_barrier(partial_value.astype(f16))]
    for k in range(1, COLS):
        sent.append(lax.ppermute(sent[0], "col", xor_pairs(COLS, k)))
    sent = [x.astype(f32) for x in sent]
    layer_out = ((sent[0] + sent[1]) + (sent[2] + sent[3])) * (1.0 / OSCALE)
    return (
        layer_out,
        readout,
        new_cell.reshape(B, H, KR, V),
        jnp.transpose(new_normal.reshape(H, KR, B), (2, 0, 1)),
        jnp.transpose(new_stab)[:, :, None],
    )


def solution(mesh):
    in_specs = (
        P("hb", None, "row", "col"),
        P("hb", None, "row"),
        P("hb", None, "row"),
        P("hb", None, "row"),
        P("hb", None, "row"),
        P("hb", None, "col"),
        P("hb", None),
        P("hb", None),
        P("hb", None, "col"),
        P(None, "col"),
        P("hb", "col", "row"),
    )
    out_specs = (
        P("hb", "row"),
        P("hb", None, "col"),
        P("hb", None, "row", "col"),
        P("hb", None, "row"),
        P("hb", None, "row"),
    )
    return jax.shard_map(local, mesh=mesh, in_specs=in_specs, out_specs=out_specs, check_vma=False)
```
